32 devices in a mesh: dp: 16 (over z, y, x), tensor: 2 (over core).
Axes of the slice: x: 2, y: 2, z: 4, core: 2. Of those that a mesh axis runs over, the one named last changes fastest.
Arguments:
- tokens: bfloat16 [2048, 1792], P('dp'), may hold values from -6 to 6
- targets: bfloat16 [2048, 1792], P('dp'), may hold values from -6 to 6
- live_mask: int32 [2048], P('dp'), may hold values from 0 to 1, as said below
- up_weight: bfloat16 [1792, 7168], P('dp', 'tensor'), may hold values from -0.125 to 0.125
- down_weight: bfloat16 [1792, 7168], P('dp', 'tensor'), may hold values from -0.0625 to 0.0625
- probe_rows: int32 [1792], replicated, may hold values from 0 to 16777215
- probe_cols: int32 [7168], P('tensor'), may hold values from 0 to 16777215
- moment: float32 [1792, 512], P('dp', 'tensor'), may hold values from 0.01 to 1
Outputs:
- hess_diag: float32 [1792, 512], P('dp', 'tensor')
- second_moment: float32 [1792, 512], P('dp', 'tensor')
- mean_loss: float32 [], replicated
The draws below stay inside these ranges and needn't reach their ends.
Inputs may be any that keep to these rules, and one draw needn't show every extreme that they name: In every aligned block of 128 tokens the first token has live_mask 1.
All inputs are finite; a program needn't handle non-finite values.
Results may differ from the reference program's by a relative error of at most 0.0023.
Values may be sent and summed in bfloat16 or wider, within the bound.
A program may use at most 128 MiB of HBM per device.

```python
import math
import jax
import jax.numpy as jnp
from jax import lax

D = 1792
FF = 7168
BLOCK = 14
TOK_DEV = 128
TOKENS = 2048


def draw_live_mask(key, part):
    group_id = jnp.arange(TOKENS) // TOK_DEV
    group_count = TOKENS // TOK_DEV
    threshold = 300 + 600 * group_id // max(group_count - 1, 1)
    dice_rolls = jax.random.randint(key, (TOKENS,), 0, 1000)
    live_rows = (dice_rolls < threshold).astype(jnp.int32)
    lead_rows = (jnp.arange(TOKENS) % TOK_DEV == 0).astype(jnp.int32)
    return jnp.maximum(live_rows, lead_rows)


def place_ends(array, rng, low, top_value):
    longest = array.shape.index(max(array.shape))
    spots = []
    for shift in (0, 1):
        where = [jax.random.randint(jax.random.fold_in(rng, axis), (), 0, length) for axis, length in enumerate(array.shape)]
        where[longest] = (where[longest] + shift) % array.shape[longest]
        spots.append(tuple(where))
    return array.at[spots[0]].set(low).at[spots[1]].set(top_value)


def block_levels(stream_key, dims, shards, low, high):
    loudness = 1.0
    for axis_at, blocks in shards:
        steps = jax.random.uniform(jax.random.fold_in(jax.random.fold_in(stream_key, 6), axis_at), (blocks,), jnp.float32, low / len(shards), high / len(shards))
        loudness = loudness * jnp.repeat(jnp.exp(steps), dims[axis_at] // blocks).reshape((-1,) + (1,) * (len(dims) - 1 - axis_at))
    return loudness


def bell_draw(rng, extent, spread, bound, split=(), held_as=jnp.bfloat16):
    level = block_levels(rng, extent, split, -0.22, 0.18) if split else 1.0
    values = jax.random.normal(rng, extent, jnp.float32) * spread * level
    return jnp.minimum(jnp.maximum(values, -bound), bound).astype(held_as)


def setup_inputs(seed: int = 0) -> dict:
    streams_of = jax.random.split(jax.random.key(seed), 9)
    return {
        "tokens": bell_draw(streams_of[0], (TOKENS, D), 1.0, 6.0, ((0, 16),)),
        "targets": bell_draw(streams_of[1], (TOKENS, D), 1.0, 6.0, ((0, 16),)),
        "live_mask": draw_live_mask(jax.random.fold_in(streams_of[8], 71), 0),
        "up_weight": bell_draw(streams_of[3], (D, FF), D ** -0.5, 0.125, ((0, 16), (1, 2))),
        "down_weight": bell_draw(streams_of[4], (D, FF), FF ** -0.5, 0.0625, ((0, 16), (1, 2))),
        "probe_rows": place_ends(jax.random.randint(streams_of[5], (D,), 0, 16777216), jax.random.fold_in(streams_of[5], 1), 0, 16777215).astype(jnp.int32),
        "probe_cols": place_ends(jax.random.randint(streams_of[6], (FF,), 0, 16777216), jax.random.fold_in(streams_of[6], 1), 0, 16777215).astype(jnp.int32),
        "moment": jnp.clip(jnp.exp(math.log(1.0) - 4.6051702 * jax.random.uniform(streams_of[7], (D, FF // BLOCK), jnp.float32) ** block_levels(streams_of[7], (D, FF // BLOCK), ((0, 16), (1, 2)), -0.2, 0.2)), 0.01, 1.0),
    }


gelu_coef = 0.7978845608028654
cubic_coef = 0.044715
beta_two = 0.999


def probe_signs(row_keys, col_keys):
    hashed = jnp.bitwise_xor(row_keys[:, None] * 747796405, col_keys[None, :])
    hashed = jnp.bitwise_xor(hashed, jnp.right_shift(hashed, 15) & 131071)
    hashed = hashed * 695872825
    hashed = jnp.bitwise_xor(hashed, jnp.right_shift(hashed, 13) & 524287)
    hashed = hashed * 739982445
    hashed = jnp.bitwise_xor(hashed, jnp.right_shift(hashed, 16) & 65535)
    parity = jnp.right_shift(hashed, 11) & 1
    return (2 * parity - 1).astype(jnp.bfloat16)


def gelu_parts(preact):
    tanh_arg = gelu_coef * (preact + cubic_coef * preact * preact * preact)
    tanh_val = jnp.tanh(tanh_arg)
    sech_sq = 1.0 - tanh_val * tanh_val
    arg_slope = gelu_coef * (1.0 + 3.0 * cubic_coef * preact * preact)
    arg_curve = gelu_coef * 6.0 * cubic_coef * preact
    gelu_value = 0.5 * preact * (1.0 + tanh_val)
    gelu_slope = 0.5 * (1.0 + tanh_val) + 0.5 * preact * sech_sq * arg_slope
    gelu_curve = sech_sq * (arg_slope - preact * tanh_val * arg_slope * arg_slope + 0.5 * preact * arg_curve)
    return gelu_value, gelu_slope, gelu_curve


def reference(tokens, targets, live_mask, up_weight, down_weight, probe_rows, probe_cols, moment):
    probe = probe_signs(probe_rows, probe_cols)
    count = jnp.sum(live_mask.astype(jnp.float32))
    group_total = TOKENS // TOK_DEV
    tok_blocks = tokens.reshape(group_total, TOK_DEV, D)
    tgt_blocks = targets.reshape(group_total, TOK_DEV, D)
    mask_blocks = live_mask.reshape(group_total, TOK_DEV)

    def token_block(running, blocks):
        acc_curv, acc_loss = running
        inputs, wanted, mask_rows = blocks
        preact = jnp.dot(inputs, up_weight, preferred_element_type=jnp.float32)
        tangent = jnp.dot(inputs, probe, preferred_element_type=jnp.float32)
        gelu_value, gelu_slope, gelu_curve = gelu_parts(preact)
        hidden = gelu_value.astype(jnp.bfloat16)
        hidden_dir = (gelu_slope * tangent).astype(jnp.bfloat16)
        outputs = jnp.dot(hidden, down_weight.T, preferred_element_type=jnp.float32)
        out_dir = jnp.dot(hidden_dir, down_weight.T, preferred_element_type=jnp.float32)
        live_rows = mask_rows.astype(jnp.float32)[:, None]
        diff = outputs - wanted.astype(jnp.float32)
        weighted = live_rows * diff
        loss_part = jnp.sum(weighted * diff)
        residual = weighted.astype(jnp.bfloat16)
        residual_dir = (live_rows * out_dir).astype(jnp.bfloat16)
        grad_h = jnp.dot(residual, down_weight, preferred_element_type=jnp.float32)
        grad_dir = jnp.dot(residual_dir, down_weight, preferred_element_type=jnp.float32)
        chain_grad = (grad_dir * gelu_slope + grad_h * gelu_curve * tangent).astype(jnp.bfloat16)
        curv_part = jnp.dot(inputs.T, chain_grad, preferred_element_type=jnp.float32)
        return (acc_curv + curv_part, acc_loss + loss_part), None

    start_state = (jnp.zeros((D, FF), jnp.float32), jnp.zeros((), jnp.float32))
    final_state, _ = lax.scan(token_block, start_state, (tok_blocks, tgt_blocks, mask_blocks))
    curv_sum, loss_sum = final_state
    hutch_terms = probe.astype(jnp.float32) * curv_sum
    hess_diag = hutch_terms.reshape(D, FF // BLOCK, BLOCK).mean(axis=-1) / count
    second_moment = beta_two * moment + (1.0 - beta_two) * hess_diag * hess_diag
    mean_loss = loss_sum / (2.0 * count)
    return hess_diag, second_moment, mean_loss
```

```python
import math
import jax
import jax.numpy as jnp
from jax import lax
from jax.sharding import Mesh, PartitionSpec as P

BLOCK = 14
FFX, TKX = "hi", "lo"

gelu_coef = 0.7978845608028654
cubic_coef = 0.044715
beta_two = 0.999


def probe_signs(row_keys, col_keys):
    hashed = jnp.bitwise_xor(row_keys[:, None] * 747796405, col_keys[None, :])
    hashed = jnp.bitwise_xor(hashed, jnp.right_shift(hashed, 15) & 131071)
    hashed = hashed * 695872825
    hashed = jnp.bitwise_xor(hashed, jnp.right_shift(hashed, 13) & 524287)
    hashed = hashed * 739982445
    hashed = jnp.bitwise_xor(hashed, jnp.right_shift(hashed, 16) & 65535)
    parity = jnp.right_shift(hashed, 11) & 1
    return (2 * parity - 1).astype(jnp.bfloat16)


def gelu_parts(preact):
    tanh_arg = gelu_coef * (preact + cubic_coef * preact * preact * preact)
    tanh_val = jnp.tanh(tanh_arg)
    sech_sq = 1.0 - tanh_val * tanh_val
    arg_slope = gelu_coef * (1.0 + 3.0 * cubic_coef * preact * preact)
    arg_curve = gelu_coef * 6.0 * cubic_coef * preact
    gelu_value = 0.5 * preact * (1.0 + tanh_val)
    gelu_slope = 0.5 * (1.0 + tanh_val) + 0.5 * preact * sech_sq * arg_slope
    gelu_curve = sech_sq * (
        arg_slope - preact * tanh_val * arg_slope * arg_slope + 0.5 * preact * arg_curve
    )
    return (gelu_value, gelu_slope, gelu_curve)


def spread(weight):
    own_rows, ff_held = weight.shape
    groups = lax.axis_size(FFX)
    cols = ff_held // groups
    pieces = lax.all_to_all(weight.reshape(own_rows, groups, cols), FFX, split_axis=1, concat_axis=0)
    full = lax.all_gather(pieces, TKX, axis=1 if FFX == "hi" else 0)
    return full.reshape(-1, cols)


def body(tokens, targets, live_mask, up_weight, down_weight, probe_rows, probe_cols, moment):
    tok_count, features = tokens.shape
    own_rows, ff_held = up_weight.shape
    groups = lax.axis_size(FFX)
    cols = ff_held // groups
    cores = lax.axis_size("tensor")
    everyone = ("hi", "lo", "tensor")
    share = tok_count // cores
    col_keys = lax.dynamic_slice_in_dim(probe_cols, lax.axis_index(FFX) * cols, cols)
    signs = probe_signs(probe_rows, col_keys)
    first = lax.axis_index("tensor") * share
    live_own = lax.dynamic_slice_in_dim(live_mask, first, share).astype(jnp.float32)
    targets_own = lax.dynamic_slice_in_dim(targets, first, share)
    all_tokens = lax.all_gather(tokens, FFX, axis=0, tiled=True)
    up_full = spread(up_weight)
    down_full = spread(down_weight)
    preact = jnp.dot(all_tokens, up_full, preferred_element_type=jnp.float32)
    tangent = jnp.dot(all_tokens, signs, preferred_element_type=jnp.float32)
    gelu_value, gelu_slope, gelu_curve = gelu_parts(preact)
    hidden = gelu_value.astype(jnp.bfloat16)
    hidden_dir = (gelu_slope * tangent).astype(jnp.bfloat16)
    stacked = jnp.stack([hidden, hidden_dir])
    projected = jnp.einsum("ntf,df->ntd", stacked, down_full, preferred_element_type=jnp.float32)
    part = projected.astype(jnp.bfloat16).reshape(2, groups * cores, share, features)
    part = lax.all_to_all(part, (FFX, "tensor"), split_axis=1, concat_axis=0)
    outputs, out_dir = jnp.sum(part.astype(jnp.float32), axis=0)
    diff = outputs - targets_own.astype(jnp.float32)
    weighted = live_own[:, None] * diff
    residual = jnp.stack([weighted, live_own[:, None] * out_dir]).astype(jnp.bfloat16)
    residual = lax.all_gather(residual, (FFX, "tensor"), axis=1, tiled=True)
    sums = lax.psum(jnp.stack([jnp.sum(weighted * diff), jnp.sum(live_own)]), everyone)
    loss_sum, total_count = sums[0], sums[1]
    grads = jnp.einsum("ntd,df->ntf", residual, down_full, preferred_element_type=jnp.float32)
    chain_grad = (grads[1] * gelu_slope + grads[0] * gelu_curve * tangent).astype(jnp.bfloat16)
    product = jnp.einsum("tr,tf->rf", all_tokens, chain_grad, preferred_element_type=jnp.float32)
    blocks = cols // BLOCK
    member = (
        lax.broadcasted_iota(jnp.int32, (cols, blocks), 0) // BLOCK
        == lax.broadcasted_iota(jnp.int32, (cols, blocks), 1)
    ).astype(jnp.float32)
    summed = jnp.dot(signs.astype(jnp.float32) * product, member, precision=lax.Precision.HIGH)
    summed = summed.reshape(lax.axis_size("hi"), lax.axis_size("lo"), own_rows, blocks)
    tk_dim = 1 if TKX == "lo" else 0
    summed = lax.all_to_all(summed, TKX, split_axis=tk_dim, concat_axis=0).sum(axis=0)
    summed = lax.all_to_all(summed, FFX, split_axis=0, concat_axis=1).reshape(own_rows, groups * blocks)
    hess_diag = summed * (1.0 / BLOCK) / total_count
    second_moment = beta_two * moment + (1.0 - beta_two) * hess_diag * hess_diag
    mean_loss = loss_sum / (2.0 * total_count)
    return (hess_diag, second_moment, mean_loss)


def solution(mesh):
    dp = mesh.shape["dp"]
    hi = math.gcd(dp, 4)
    split = Mesh(mesh.devices.reshape(hi, dp // hi, mesh.shape["tensor"]), ("hi", "lo", "tensor"))
    rows = ("hi", "lo")
    placed = (
        P(rows, None),
        P(rows, None),
        P(rows),
        P(rows, "tensor"),
        P(rows, "tensor"),
        P(),
        P("tensor"),
        P(rows, "tensor"),
    )
    return jax.shard_map(
        body,
        mesh=split,
        in_specs=placed,
        out_specs=(P(rows, "tensor"), P(rows, "tensor"), P()),
        check_vma=False,
    )
```

```python
import functools
import math
import jax
import jax.numpy as jnp
from jax import lax
from jax.experimental import pallas as pl
from jax.experimental.pallas import tpu as pltpu
from jax.sharding import Mesh, PartitionSpec as P

BLOCK = 14

gelu_coef = 0.7978845608028654
cubic_coef = 0.044715
beta_two = 0.999


def probe_signs(row_keys, col_keys):
    hashed = jnp.bitwise_xor(row_keys[:, None] * 747796405, col_keys[None, :])
    hashed = jnp.bitwise_xor(hashed, jnp.right_shift(hashed, 15) & 131071)
    hashed = hashed * 695872825
    hashed = jnp.bitwise_xor(hashed, jnp.right_shift(hashed, 13) & 524287)
    hashed = hashed * 739982445
    hashed = jnp.bitwise_xor(hashed, jnp.right_shift(hashed, 16) & 65535)
    parity = jnp.right_shift(hashed, 11) & 1
    return (2 * parity - 1).astype(jnp.bfloat16)


def gelu_parts(preact):
    tanh_arg = gelu_coef * (preact + cubic_coef * preact * preact * preact)
    tanh_val = jnp.tanh(tanh_arg)
    sech_sq = 1.0 - tanh_val * tanh_val
    arg_slope = gelu_coef * (1.0 + 3.0 * cubic_coef * preact * preact)
    arg_curve = gelu_coef * 6.0 * cubic_coef * preact
    gelu_value = 0.5 * preact * (1.0 + tanh_val)
    gelu_slope = 0.5 * (1.0 + tanh_val) + 0.5 * preact * sech_sq * arg_slope
    gelu_curve = sech_sq * (
        arg_slope - preact * tanh_val * arg_slope * arg_slope + 0.5 * preact * arg_curve
    )
    return (gelu_value, gelu_slope, gelu_curve)


MESH = pl.DeviceIdType.MESH
ANY = pl.BlockSpec(memory_space=pl.ANY)
VMEM = pl.BlockSpec(memory_space=pltpu.VMEM)


def remote(src, dst, send_sem, recv_sem, device):
    return pltpu.make_async_remote_copy(
        src_ref=src, dst_ref=dst, send_sem=send_sem, recv_sem=recv_sem, device_id=device, device_id_type=MESH
    )


def gather_kernel(
    n, groups, tok_ref, up_ref, down_ref, tok_all, up_all, down_all,
    own_sem, tok_send, tok_recv, swap_send, swap_recv, line_send, line_recv,
):
    z, g, c = lax.axis_index("hi"), lax.axis_index("lo"), lax.axis_index("tensor")
    cols = up_all.shape[3]
    barrier = pltpu.get_barrier_semaphore()
    for d in range(1, groups):
        pl.semaphore_signal(barrier, inc=1, device_id=(z, lax.rem(g + d, groups), c), device_id_type=MESH)

    for side in (1, n - 1):
        pl.semaphore_signal(barrier, inc=1, device_id=(lax.rem(z + side, n), g, c), device_id_type=MESH)
    pl.semaphore_wait(barrier, groups + 1)

    def cut(ref, at):
        return ref.at[:, pl.ds(pl.multiple_of(at * cols, cols), cols)]

    held = ((up_ref, up_all), (down_ref, down_all))

    def swap(w, d):
        to = lax.rem(g + d, groups)
        return remote(cut(held[w][0], to), held[w][1].at[z, g], swap_send.at[w, d - 1], swap_recv.at[w, d - 1], (z, to, c))

    def swapped(w, d):
        came = lax.rem(g + groups - d, groups)
        return remote(cut(held[w][0], came), held[w][1].at[z, came], swap_send.at[w, d - 1], swap_recv.at[w, d - 1], (z, came, c))

    def token_send(d):
        to = lax.rem(g + d, groups)
        return remote(tok_ref, tok_all.at[g], tok_send.at[d - 1], tok_recv.at[d - 1], (z, to, c))

    def token_got(d):
        came = lax.rem(g + groups - d, groups)
        return remote(tok_ref, tok_all.at[came], tok_send.at[d - 1], tok_recv.at[d - 1], (z, came, c))

    def hop(w, way, d, s):
        step = 1 if way == 0 else -1
        slot = held[w][1].at[z - step * s, lax.rem(g + groups - d, groups)]
        return remote(slot, slot, line_send.at[w, way, d, s], line_recv.at[w, way, d, s], (z + step, g, c))

    def arrival(w, way, d, s):
        step = 1 if way == 0 else -1
        slot = held[w][1].at[z - step * s, lax.rem(g + groups - d, groups)]
        return remote(slot, slot, line_send.at[w, way, d, s - 1], line_recv.at[w, way, d, s - 1], (z - step, g, c))

    def goes(way, s):
        if way == 0:
            return (z < n - 1) & (z - s >= 0)
        return (z > 0) & (z + s <= n - 1)

    def comes(way, s):
        return z - s >= 0 if way == 0 else z + s <= n - 1

    owns = [pltpu.make_async_copy(cut(src, g), dst.at[z, g], own_sem.at[w]) for w, (src, dst) in enumerate(held)]
    owns.append(pltpu.make_async_copy(tok_ref, tok_all.at[g], own_sem.at[2]))
    for copy in owns:
        copy.start()
    for d in range(1, groups):
        swap(0, d).start()
    for d in range(1, groups):
        token_send(d).start()
    for d in range(1, groups):
        swap(1, d).start()
    for w in range(2):
        for d in range(groups):
            if d == 0:
                owns[w].wait()
            else:
                swapped(w, d).wait_recv()
            for way in range(2):
                @pl.when(goes(way, 0))
                def _():
                    hop(w, way, d, 0).start()

        @pl.loop(1, n)
        def _(s):
            for d in range(groups):
                for way in range(2):
                    @pl.when(comes(way, s))
                    def _():
                        arrival(w, way, d, s).wait_recv()

                    @pl.when(goes(way, s))
                    def _():
                        hop(w, way, d, s).start()

    owns[2].wait()
    for d in range(1, groups):
        token_send(d).wait_send()
        token_got(d).wait_recv()
    for w in range(2):
        for d in range(1, groups):
            swap(w, d).wait_send()

        @pl.loop(0, n - 1)
        def _(s):
            for d in range(groups):
                for way in range(2):
                    @pl.when(goes(way, s))
                    def _():
                        hop(w, way, d, s).wait_send()


def gather(n, groups, tokens, up_weight, down_weight):
    tok_count, features = tokens.shape
    own_rows, ff_held = up_weight.shape
    full = jax.ShapeDtypeStruct((n, groups, own_rows, ff_held // groups), up_weight.dtype)
    dma = pltpu.SemaphoreType.DMA
    return pl.pallas_call(
        functools.partial(gather_kernel, n, groups),
        name="gather",
        out_shape=(jax.ShapeDtypeStruct((groups, tok_count, features), tokens.dtype), full, full),
        in_specs=[ANY] * 3,
        out_specs=(ANY,) * 3,
        scratch_shapes=[
            dma((3,)), dma((groups - 1,)), dma((groups - 1,)), dma((2, groups - 1)), dma((2, groups - 1)),
            dma((2, 2, groups, n - 1)), dma((2, 2, groups, n - 1)),
        ],
        compiler_params=pltpu.CompilerParams(collective_id=0, has_side_effects=True),
    )(tokens, up_weight, down_weight)


def residual_kernel(
    groups, cores, out_ref, dir_ref, targets_ref, live_ref, res_all, tile_all,
    half_out, half_dir, send_out, send_dir, got_out, got_dir,
    half_send, half_recv, part_send, part_recv, res_send, res_recv, pass_send, pass_recv, tile_send, tile_recv,
):
    z, g, c = lax.axis_index("hi"), lax.axis_index("lo"), lax.axis_index("tensor")
    twin = 1 - c
    barrier = pltpu.get_barrier_semaphore()
    others = [(d, e) for d in range(groups) for e in range(cores) if (d, e) != (0, 0)]

    def at(d, e):
        return (z, lax.rem(g + d, groups), lax.rem(c + e, cores))

    def back(d, e):
        return (z, lax.rem(g + groups - d, groups), lax.rem(c + cores - e, cores))

    for d, e in others:
        pl.semaphore_signal(barrier, inc=1, device_id=at(d, e), device_id_type=MESH)
    pl.semaphore_wait(barrier, len(others))

    def halves(d):
        to = lax.rem(g + d, groups)
        return (
            remote(out_ref.at[to, twin], half_out.at[d], half_send.at[0, d], half_recv.at[0, d], (z, g, twin)),
            remote(dir_ref.at[to, twin], half_dir.at[d], half_send.at[1, d], half_recv.at[1, d], (z, g, twin)),
        )

    def parts(d):
        return (
            remote(send_out.at[d], got_out.at[d - 1], part_send.at[0, d - 1], part_recv.at[0, d - 1], at(d, 0)),
            remote(send_dir.at[d], got_dir.at[d - 1], part_send.at[1, d - 1], part_recv.at[1, d - 1], at(d, 0)),
        )

    order = list(range(1, groups)) + [0]
    for d in order:
        for copy in halves(d):
            copy.start()
    for d in order:
        to = lax.rem(g + d, groups)
        for copy in halves(d):
            copy.wait_recv()
        total = out_ref[to, c].astype(jnp.float32) + half_out[d].astype(jnp.float32)
        send_out[d] = total.astype(jnp.bfloat16)
        send_dir[d] = dir_ref[to, c] + half_dir[d]
        if d:
            for copy in parts(d):
                copy.start()
    outputs = total
    out_dir = send_dir[0]
    for d in range(1, groups):
        for copy in parts(d):
            copy.wait_recv()
        outputs += got_out[d - 1].astype(jnp.float32)
        out_dir += got_dir[d - 1]
    live = live_ref[...]
    diff = outputs - targets_ref[...].astype(jnp.float32)
    weighted = live * diff
    res_all[0, g, c] = weighted.astype(jnp.bfloat16)
    res_all[1, g, c] = (live * out_dir).astype(jnp.bfloat16)
    loss = jnp.sum(weighted * diff, keepdims=True)
    count = jnp.sum(live, keepdims=True)
    tile_all[g, c] = jnp.where(lax.broadcasted_iota(jnp.int32, tile_all.shape[2:], 0) == 0, loss, count)

    def sent(d):
        slot = res_all.at[:, g, c]
        return remote(slot, slot, res_send.at[d], res_recv.at[d], at(d, 0) if d else (z, g, twin))

    def received(d):
        slot = res_all.at[:, lax.rem(g + groups - d, groups), c] if d else res_all.at[:, g, twin]
        return remote(slot, slot, res_send.at[d], res_recv.at[d], back(d, 0) if d else (z, g, twin))

    def passed(d, core):
        slot = res_all.at[:, lax.rem(g + groups - d, groups), core]
        return remote(slot, slot, pass_send.at[d - 1], pass_recv.at[d - 1], (z, g, twin))

    def tile(i, core_from, place):
        slot = tile_all.at[core_from[1], core_from[2]]
        return remote(slot, slot, tile_send.at[i], tile_recv.at[i], place)

    for d in order:
        sent(d).start()
    for i, (d, e) in enumerate(others):
        tile(i, (z, g, c), at(d, e)).start()
    for d in range(1, groups):
        received(d).wait_recv()
        passed(d, c).start()
    received(0).wait_recv()
    for i, (d, e) in enumerate(others):
        tile(i, back(d, e), back(d, e)).wait_recv()
    for d in range(1, groups):
        passed(d, twin).wait_recv()
    for d in range(groups):
        for copy in halves(d):
            copy.wait_send()
        sent(d).wait_send()
        if d:
            for copy in parts(d):
                copy.wait_send()
            passed(d, c).wait_send()
    for i, (d, e) in enumerate(others):
        tile(i, (z, g, c), at(d, e)).wait_send()


def exchange(groups, cores, out_part, dir_part, targets, live):
    share, features = targets.shape
    dma = pltpu.SemaphoreType.DMA
    bf, f32 = jnp.bfloat16, jnp.float32
    return pl.pallas_call(
        functools.partial(residual_kernel, groups, cores),
        name="residual",
        out_shape=(
            jax.ShapeDtypeStruct((2, groups, cores, share, features), bf),
            jax.ShapeDtypeStruct((groups, cores, 8, 128), f32),
        ),
        in_specs=[VMEM] * 4,
        out_specs=(VMEM,) * 2,
        scratch_shapes=[
            pltpu.VMEM((groups, share, features), bf), pltpu.VMEM((groups, share, features), f32),
            pltpu.VMEM((groups, share, features), bf), pltpu.VMEM((groups, share, features), f32),
            pltpu.VMEM((groups - 1, share, features), bf), pltpu.VMEM((groups - 1, share, features), f32),
            dma((2, groups)), dma((2, groups)), dma((2, groups - 1)), dma((2, groups - 1)),
            dma((groups,)), dma((groups,)), dma((groups - 1,)), dma((groups - 1,)),
            dma((groups * cores - 1,)), dma((groups * cores - 1,)),
        ],
        compiler_params=pltpu.CompilerParams(collective_id=1, has_side_effects=True),
    )(out_part, dir_part, targets, live)


def reduce_kernel(
    n, groups, part_ref, tile_ref, out_ref, sums_ref, got, got_tile, total,
    line_send, line_recv, tile_send, tile_recv, swap_send, swap_recv,
):
    z, g, c = lax.axis_index("hi"), lax.axis_index("lo"), lax.axis_index("tensor")
    barrier = pltpu.get_barrier_semaphore()
    for d in range(1, groups):
        pl.semaphore_signal(barrier, inc=1, device_id=(z, lax.rem(g + d, groups), c), device_id_type=MESH)
    for s in range(1, n):
        pl.semaphore_signal(barrier, inc=1, device_id=(lax.rem(z + s, n), g, c), device_id_type=MESH)
    pl.semaphore_wait(barrier, groups + n - 2)

    def line(s):
        to = lax.rem(z + s, n)
        return (
            remote(part_ref.at[to], got.at[s - 1], line_send.at[s - 1], line_recv.at[s - 1], (to, g, c)),
            remote(tile_ref, got_tile.at[s - 1], tile_send.at[s - 1], tile_recv.at[s - 1], (to, g, c)),
        )

    def swap(d):
        to = lax.rem(g + d, groups)
        return remote(total.at[to], out_ref.at[g], swap_send.at[d - 1], swap_recv.at[d - 1], (z, to, c))

    def swapped(d):
        came = lax.rem(g + groups - d, groups)
        return remote(total.at[came], out_ref.at[came], swap_send.at[d - 1], swap_recv.at[d - 1], (z, came, c))

    for s in range(1, n):
        for copy in line(s):
            copy.start()
    acc = part_ref[z]
    sums = tile_ref[...]
    for s in range(1, n):
        for copy in line(s):
            copy.wait_recv()
        acc += got[s - 1]
        sums += got_tile[s - 1]
    total[...] = acc
    sums_ref[...] = sums
    for d in range(1, groups):
        swap(d).start()
    out_ref[g] = total[g]
    for d in range(1, groups):
        swapped(d).wait_recv()
    for d in range(1, groups):
        swap(d).wait_send()
    for s in range(1, n):
        for copy in line(s):
            copy.wait_send()


def reduce_rows(n, groups, part, tile):
    own_rows, blocks = part.shape[2:]
    dma = pltpu.SemaphoreType.DMA
    shape = (groups, own_rows, blocks)
    return pl.pallas_call(
        functools.partial(reduce_kernel, n, groups),
        name="reduce_rows",
        out_shape=(jax.ShapeDtypeStruct(shape, part.dtype), jax.ShapeDtypeStruct(tile.shape, tile.dtype)),
        in_specs=[VMEM] * 2,
        out_specs=(VMEM,) * 2,
        scratch_shapes=[
            pltpu.VMEM((n - 1,) + shape, part.dtype), pltpu.VMEM((n - 1,) + tile.shape, tile.dtype),
            pltpu.VMEM(shape, part.dtype),
            dma((n - 1,)), dma((n - 1,)), dma((n - 1,)), dma((n - 1,)), dma((groups - 1,)), dma((groups - 1,)),
        ],
        compiler_params=pltpu.CompilerParams(collective_id=2, has_side_effects=True),
    )(part, tile)


def body(tokens, targets, live_mask, up_weight, down_weight, probe_rows, probe_cols, moment):
    tok_count, features = tokens.shape
    own_rows, ff_held = up_weight.shape
    n, groups, cores = lax.axis_size("hi"), lax.axis_size("lo"), lax.axis_size("tensor")
    cols = ff_held // groups
    share = tok_count // cores
    col_keys = lax.dynamic_slice_in_dim(probe_cols, lax.axis_index("lo") * cols, cols)
    signs = probe_signs(probe_rows, col_keys)
    first = lax.axis_index("tensor") * share
    live_own = lax.dynamic_slice_in_dim(live_mask, first, share).astype(jnp.float32)[:, None]
    targets_own = lax.dynamic_slice_in_dim(targets, first, share)
    all_tokens, up_full, down_full = gather(n, groups, tokens, up_weight, down_weight)
    all_tokens = all_tokens.reshape(-1, features)
    up_full = up_full.reshape(features, cols)
    down_full = down_full.reshape(features, cols)
    preact = jnp.dot(all_tokens, up_full, preferred_element_type=jnp.float32)
    tangent = jnp.dot(all_tokens, signs, preferred_element_type=jnp.float32)
    gelu_value, gelu_slope, gelu_curve = gelu_parts(preact)
    hidden = gelu_value.astype(jnp.bfloat16)
    hidden_dir = (gelu_slope * tangent).astype(jnp.bfloat16)
    dims = (((1,), (1,)), ((), ()))
    out_part = lax.dot_general(hidden, down_full, dims, preferred_element_type=jnp.float32).astype(jnp.bfloat16)
    dir_part = lax.dot_general(hidden_dir, down_full, dims, preferred_element_type=jnp.float32)
    split = (groups, cores, share, features)
    residual, tiles = exchange(groups, cores, out_part.reshape(split), dir_part.reshape(split), targets_own, live_own)
    residual = residual.reshape(2, -1, features)
    tile = jnp.sum(tiles, axis=(0, 1))
    grads = jnp.einsum("ntd,df->ntf", residual, down_full, preferred_element_type=jnp.float32)
    chain_grad = (grads[1] * gelu_slope + grads[0] * gelu_curve * tangent).astype(jnp.bfloat16)
    product = jnp.einsum("tr,tf->rf", all_tokens, chain_grad, preferred_element_type=jnp.float32)
    blocks = cols // BLOCK
    member = (
        lax.broadcasted_iota(jnp.int32, (cols, blocks), 0) // BLOCK
        == lax.broadcasted_iota(jnp.int32, (cols, blocks), 1)
    ).astype(jnp.float32)
    summed = jnp.dot(signs.astype(jnp.float32) * product, member, precision=lax.Precision.HIGH)
    rows, sums = reduce_rows(n, groups, summed.reshape(n, groups, own_rows, blocks), tile)
    loss_sum, total_count = sums[0, 0], sums[1, 0]
    summed = rows.transpose(1, 0, 2).reshape(own_rows, groups * blocks)
    hess_diag = summed * (1.0 / BLOCK) / total_count
    second_moment = beta_two * moment + (1.0 - beta_two) * hess_diag * hess_diag
    mean_loss = loss_sum / (2.0 * total_count)
    return (hess_diag, second_moment, mean_loss)


def solution(mesh):
    dp = mesh.shape["dp"]
    lo = math.gcd(dp, 4)
    split = Mesh(mesh.devices.reshape(dp // lo, lo, mesh.shape["tensor"]), ("hi", "lo", "tensor"))
    rows = ("hi", "lo")
    placed = (
        P(rows, None),
        P(rows, None),
        P(rows),
        P(rows, "tensor"),
        P(rows, "tensor"),
        P(),
        P("tensor"),
        P(rows, "tensor"),
    )
    return jax.shard_map(
        body,
        mesh=split,
        in_specs=placed,
        out_specs=(P(rows, "tensor"), P(rows, "tensor"), P()),
        check_vma=False,
    )
```

```python
import functools
import jax
import jax.numpy as jnp
from jax import lax
from jax.experimental import pallas as pl
from jax.experimental.pallas import tpu as pltpu
from jax.sharding import Mesh, PartitionSpec as P

BLOCK = 14

gelu_coef = 0.7978845608028654
cubic_coef = 0.044715
beta_two = 0.999


def probe_signs(row_keys, col_keys):
    hashed = jnp.bitwise_xor(row_keys[:, None] * 747796405, col_keys[None, :])
    hashed = jnp.bitwise_xor(hashed, jnp.right_shift(hashed, 15) & 131071)
    hashed = hashed * 695872825
    hashed = jnp.bitwise_xor(hashed, jnp.right_shift(hashed, 13) & 524287)
    hashed = hashed * 739982445
    hashed = jnp.bitwise_xor(hashed, jnp.right_shift(hashed, 16) & 65535)
    parity = jnp.right_shift(hashed, 11) & 1
    return (2 * parity - 1).astype(jnp.bfloat16)


def gelu_parts(preact):
    tanh_arg = gelu_coef * (preact + cubic_coef * preact * preact * preact)
    tanh_val = jnp.tanh(tanh_arg)
    sech_sq = 1.0 - tanh_val * tanh_val
    arg_slope = gelu_coef * (1.0 + 3.0 * cubic_coef * preact * preact)
    arg_curve = gelu_coef * 6.0 * cubic_coef * preact
    gelu_value = 0.5 * preact * (1.0 + tanh_val)
    gelu_slope = 0.5 * (1.0 + tanh_val) + 0.5 * preact * sech_sq * arg_slope
    gelu_curve = sech_sq * (
        arg_slope - preact * tanh_val * arg_slope * arg_slope + 0.5 * preact * arg_curve
    )
    return (gelu_value, gelu_slope, gelu_curve)


AXES = ("a", "b", "e", "f", "tensor")
MESH = pl.DeviceIdType.MESH
ANY = pl.BlockSpec(memory_space=pl.ANY)
VMEM = pl.BlockSpec(memory_space=pltpu.VMEM)


def remote(src, dst, send_sem, recv_sem, device):
    return pltpu.make_async_remote_copy(
        src_ref=src, dst_ref=dst, send_sem=send_sem, recv_sem=recv_sem, device_id=device, device_id_type=MESH
    )


def offsets(*sizes):
    found = [()]
    for size in sizes:
        found = [head + (step,) for head in found for step in range(size)]
    return found


def moved(at, step, size, way):
    return lax.rem(at + step if way > 0 else at + size - step, size)


def gather_kernel(
    sizes, tok_ref, up_ref, down_ref, tok_all, up_all, down_all,
    own_sem, tok_send, tok_recv, swap_send, swap_recv, far_send, far_recv, near_send, near_recv,
):
    na, nb, ne, nf = sizes
    a, b, e, f, c = (lax.axis_index(name) for name in AXES)
    cols = up_all.shape[5]
    plane = offsets(nb, nf)
    barrier = pltpu.get_barrier_semaphore()

    def peer(d, way):
        return (a, moved(b, plane[d][0], nb, way), e, moved(f, plane[d][1], nf, way), c)

    def far(s, way):
        return (moved(a, s, na, way), b, e, f, c)

    def near(t, way):
        return (a, b, moved(e, t, ne, way), f, c)

    friends = [peer(d, 1) for d in range(1, len(plane))]
    friends += [far(s, 1) for s in range(1, na)] + [near(t, 1) for t in range(1, ne)]
    for place in friends:
        pl.semaphore_signal(barrier, inc=1, device_id=place, device_id_type=MESH)
    pl.semaphore_wait(barrier, len(friends))

    held = ((up_ref, up_all), (down_ref, down_all))

    def cut(w, place):
        return held[w][0].at[:, pl.ds(pl.multiple_of((place[1] * nf + place[3]) * cols, cols), cols)]

    def swap(w, d):
        to = peer(d, 1)
        sems = swap_send.at[w, d - 1], swap_recv.at[w, d - 1]
        return remote(cut(w, to), held[w][1].at[a, b, e, f], *sems, to)

    def swapped(w, d):
        came = peer(d, -1)
        sems = swap_send.at[w, d - 1], swap_recv.at[w, d - 1]
        return remote(cut(w, came), held[w][1].at[a, came[1], e, came[3]], *sems, came)

    def token(d, way):
        place = peer(d, way)
        slot = tok_all.at[b, f] if way > 0 else tok_all.at[place[1], place[3]]
        return remote(tok_ref, slot, tok_send.at[d - 1], tok_recv.at[d - 1], place)

    def chunk(w, d, at_a, at_e):
        came = peer(d, -1)
        return held[w][1].at[at_a, came[1], at_e, came[3]]

    def far_hop(w, d, s, way):
        slot = chunk(w, d, a if way > 0 else moved(a, s, na, -1), e)
        return remote(slot, slot, far_send.at[w, d, s - 1], far_recv.at[w, d, s - 1], far(s, way))

    def near_hop(w, d, s, t, way):
        slot = chunk(w, d, moved(a, s, na, -1), e if way > 0 else moved(e, t, ne, -1))
        return remote(slot, slot, near_send.at[w, d, s, t - 1], near_recv.at[w, d, s, t - 1], near(t, way))

    owns = [pltpu.make_async_copy(cut(w, (a, b, e, f)), held[w][1].at[a, b, e, f], own_sem.at[w]) for w in range(2)]
    owns.append(pltpu.make_async_copy(tok_ref, tok_all.at[b, f], own_sem.at[2]))
    for copy in owns:
        copy.start()
    for d in range(1, len(plane)):
        swap(0, d).start()
    for d in range(1, len(plane)):
        swap(1, d).start()
    for d in range(1, len(plane)):
        token(d, 1).start()
    for w in range(2):
        for d in range(len(plane)):
            if d == 0:
                owns[w].wait()
            else:
                swapped(w, d).wait_recv()

            @pl.loop(1, na)
            def _(s):
                far_hop(w, d, s, 1).start()

            for t in range(1, ne):
                near_hop(w, d, 0, t, 1).start()
    for w in range(2):
        for d in range(len(plane)):
            @pl.loop(1, na)
            def _(s):
                far_hop(w, d, s, -1).wait_recv()
                for t in range(1, ne):
                    near_hop(w, d, s, t, 1).start()

    owns[2].wait()
    for d in range(1, len(plane)):
        token(d, -1).wait_recv()
        token(d, 1).wait_send()
    for w in range(2):
        for d in range(1, len(plane)):
            swap(w, d).wait_send()
        for d in range(len(plane)):
            @pl.loop(0, na)
            def _(s):
                for t in range(1, ne):
                    near_hop(w, d, s, t, -1).wait_recv()
                    near_hop(w, d, s, t, 1).wait_send()

            @pl.loop(1, na)
            def _(s):
                far_hop(w, d, s, 1).wait_send()


def gather(sizes, tokens, up_weight, down_weight):
    na, nb, ne, nf = sizes
    tok_count, features = tokens.shape
    own_rows, ff_held = up_weight.shape
    groups = nb * nf
    full = jax.ShapeDtypeStruct(sizes + (own_rows, ff_held // groups), up_weight.dtype)
    dma = pltpu.SemaphoreType.DMA
    return pl.pallas_call(
        functools.partial(gather_kernel, sizes),
        name="gather",
        out_shape=(jax.ShapeDtypeStruct((nb, nf, tok_count, features), tokens.dtype), full, full),
        in_specs=[ANY] * 3,
        out_specs=(ANY,) * 3,
        scratch_shapes=[
            dma((3,)), dma((groups - 1,)), dma((groups - 1,)), dma((2, groups - 1)), dma((2, groups - 1)),
            dma((2, groups, na - 1)), dma((2, groups, na - 1)),
            dma((2, groups, na, ne - 1)), dma((2, groups, na, ne - 1)),
        ],
        compiler_params=pltpu.CompilerParams(collective_id=0, has_side_effects=True),
    )(tokens, up_weight, down_weight)


def residual_kernel(
    sizes, cores, out_ref, dir_ref, targets_ref, live_ref, res_all, tile_all,
    half_out, half_dir, send_out, send_dir, got_out, got_dir,
    half_send, half_recv, part_send, part_recv, res_send, res_recv, pass_send, pass_recv, tile_send, tile_recv,
):
    na, nb, ne, nf = sizes
    a, b, e, f, c = (lax.axis_index(name) for name in AXES)
    plane = offsets(nb, nf)
    groups = len(plane)
    twin = 1 - c
    g = b * nf + f
    twin_at = (a, b, e, f, twin)
    barrier = pltpu.get_barrier_semaphore()
    others = [(d, k) for d in range(groups) for k in range(cores) if (d, k) != (0, 0)]

    def at(d, k, way=1):
        return (a, moved(b, plane[d][0], nb, way), e, moved(f, plane[d][1], nf, way), moved(c, k, cores, way))

    def back(d, k):
        return at(d, k, -1)

    def spot(d, way):
        place = at(d, 0, way)
        return place[1] * nf + place[3]

    for d, k in others:
        pl.semaphore_signal(barrier, inc=1, device_id=at(d, k), device_id_type=MESH)
    pl.semaphore_wait(barrier, len(others))

    def halves(d):
        to = spot(d, 1)
        return (
            remote(out_ref.at[to, twin], half_out.at[d], half_send.at[0, d], half_recv.at[0, d], twin_at),
            remote(dir_ref.at[to, twin], half_dir.at[d], half_send.at[1, d], half_recv.at[1, d], twin_at),
        )

    def parts(d):
        return (
            remote(send_out.at[d], got_out.at[d - 1], part_send.at[0, d - 1], part_recv.at[0, d - 1], at(d, 0)),
            remote(send_dir.at[d], got_dir.at[d - 1], part_send.at[1, d - 1], part_recv.at[1, d - 1], at(d, 0)),
        )

    order = list(range(1, groups)) + [0]
    for d in order:
        for copy in halves(d):
            copy.start()
    for d in order:
        to = spot(d, 1)
        for copy in halves(d):
            copy.wait_recv()
        total = out_ref[to, c].astype(jnp.float32) + half_out[d].astype(jnp.float32)
        send_out[d] = total.astype(jnp.bfloat16)
        send_dir[d] = dir_ref[to, c] + half_dir[d]
        if d:
            for copy in parts(d):
                copy.start()
    outputs = total
    out_dir = send_dir[0]
    for d in range(1, groups):
        for copy in parts(d):
            copy.wait_recv()
        outputs += got_out[d - 1].astype(jnp.float32)
        out_dir += got_dir[d - 1]
    live = live_ref[...]
    diff = outputs - targets_ref[...].astype(jnp.float32)
    weighted = live * diff
    res_all[0, g, c] = weighted.astype(jnp.bfloat16)
    res_all[1, g, c] = (live * out_dir).astype(jnp.bfloat16)
    loss = jnp.sum(weighted * diff, keepdims=True)
    count = jnp.sum(live, keepdims=True)
    tile_all[g, c] = jnp.where(lax.broadcasted_iota(jnp.int32, tile_all.shape[2:], 0) == 0, loss, count)

    def sent(d):
        slot = res_all.at[:, g, c]
        return remote(slot, slot, res_send.at[d], res_recv.at[d], at(d, 0) if d else twin_at)

    def received(d):
        slot = res_all.at[:, spot(d, -1), c] if d else res_all.at[:, g, twin]
        return remote(slot, slot, res_send.at[d], res_recv.at[d], back(d, 0) if d else twin_at)

    def passed(d, core):
        slot = res_all.at[:, spot(d, -1), core]
        return remote(slot, slot, pass_send.at[d - 1], pass_recv.at[d - 1], twin_at)

    def tile(i, source, place):
        slot = tile_all.at[source[1] * nf + source[3], source[4]]
        return remote(slot, slot, tile_send.at[i], tile_recv.at[i], place)

    for d in order:
        sent(d).start()
    for i, (d, k) in enumerate(others):
        tile(i, (a, b, e, f, c), at(d, k)).start()
    for d in range(1, groups):
        received(d).wait_recv()
        passed(d, c).start()
    received(0).wait_recv()
    for i, (d, k) in enumerate(others):
        tile(i, back(d, k), back(d, k)).wait_recv()
    for d in range(1, groups):
        passed(d, twin).wait_recv()
    for d in range(groups):
        for copy in halves(d):
            copy.wait_send()
        sent(d).wait_send()
        if d:
            for copy in parts(d):
                copy.wait_send()
            passed(d, c).wait_send()
    for i, (d, k) in enumerate(others):
        tile(i, (a, b, e, f, c), at(d, k)).wait_send()


def exchange(sizes, cores, out_part, dir_part, targets, live):
    groups = sizes[1] * sizes[3]
    share, features = targets.shape
    dma = pltpu.SemaphoreType.DMA
    bf, f32 = jnp.bfloat16, jnp.float32
    return pl.pallas_call(
        functools.partial(residual_kernel, sizes, cores),
        name="residual",
        out_shape=(
            jax.ShapeDtypeStruct((2, groups, cores, share, features), bf),
            jax.ShapeDtypeStruct((groups, cores, 8, 128), f32),
        ),
        in_specs=[VMEM] * 4,
        out_specs=(VMEM,) * 2,
        scratch_shapes=[
            pltpu.VMEM((groups, share, features), bf), pltpu.VMEM((groups, share, features), f32),
            pltpu.VMEM((groups, share, features), bf), pltpu.VMEM((groups, share, features), f32),
            pltpu.VMEM((groups - 1, share, features), bf), pltpu.VMEM((groups - 1, share, features), f32),
            dma((2, groups)), dma((2, groups)), dma((2, groups - 1)), dma((2, groups - 1)),
            dma((groups,)), dma((groups,)), dma((groups - 1,)), dma((groups - 1,)),
            dma((groups * cores - 1,)), dma((groups * cores - 1,)),
        ],
        compiler_params=pltpu.CompilerParams(collective_id=1, has_side_effects=True),
    )(out_part, dir_part, targets, live)


def reduce_kernel(
    sizes, part_ref, tile_ref, out_ref, sums_ref, got, got_tile, total,
    line_send, line_recv, tile_send, tile_recv, swap_send, swap_recv,
):
    na, nb, ne, nf = sizes
    a, b, e, f, c = (lax.axis_index(name) for name in AXES)
    plane, fans = offsets(nb, nf), offsets(na, ne)
    barrier = pltpu.get_barrier_semaphore()

    def peer(d, way):
        return (a, moved(b, plane[d][0], nb, way), e, moved(f, plane[d][1], nf, way), c)

    def fan(s):
        return (moved(a, fans[s][0], na, 1), b, moved(e, fans[s][1], ne, 1), f, c)

    friends = [peer(d, 1) for d in range(1, len(plane))] + [fan(s) for s in range(1, len(fans))]
    for place in friends:
        pl.semaphore_signal(barrier, inc=1, device_id=place, device_id_type=MESH)
    pl.semaphore_wait(barrier, len(friends))

    def line(s):
        to = fan(s)
        return (
            remote(part_ref.at[to[0], :, to[2]], got.at[s - 1], line_send.at[s - 1], line_recv.at[s - 1], to),
            remote(tile_ref, got_tile.at[s - 1], tile_send.at[s - 1], tile_recv.at[s - 1], to),
        )

    def swap(d, way):
        place = peer(d, way)
        slot = out_ref.at[b, f] if way > 0 else out_ref.at[place[1], place[3]]
        return remote(total.at[place[1], place[3]], slot, swap_send.at[d - 1], swap_recv.at[d - 1], place)

    for s in range(1, len(fans)):
        for copy in line(s):
            copy.start()
    acc = part_ref[a, :, e]
    sums = tile_ref[...]
    for s in range(1, len(fans)):
        for copy in line(s):
            copy.wait_recv()
        acc += got[s - 1]
        sums += got_tile[s - 1]
    total[...] = acc
    sums_ref[...] = sums
    for d in range(1, len(plane)):
        swap(d, 1).start()
    out_ref[b, f] = total[b, f]
    for d in range(1, len(plane)):
        swap(d, -1).wait_recv()
    for d in range(1, len(plane)):
        swap(d, 1).wait_send()
    for s in range(1, len(fans)):
        for copy in line(s):
            copy.wait_send()


def reduce_rows(sizes, part, tile):
    na, nb, ne, nf = sizes
    dma = pltpu.SemaphoreType.DMA
    shape = (nb, nf) + part.shape[4:]
    peers, groups = na * ne - 1, nb * nf
    return pl.pallas_call(
        functools.partial(reduce_kernel, sizes),
        name="reduce_rows",
        out_shape=(jax.ShapeDtypeStruct(shape, part.dtype), jax.ShapeDtypeStruct(tile.shape, tile.dtype)),
        in_specs=[VMEM] * 2,
        out_specs=(VMEM,) * 2,
        scratch_shapes=[
            pltpu.VMEM((peers,) + shape, part.dtype), pltpu.VMEM((peers,) + tile.shape, tile.dtype),
            pltpu.VMEM(shape, part.dtype),
            dma((peers,)), dma((peers,)), dma((peers,)), dma((peers,)), dma((groups - 1,)), dma((groups - 1,)),
        ],
        compiler_params=pltpu.CompilerParams(collective_id=2, has_side_effects=True),
    )(part, tile)


def body(tokens, targets, live_mask, up_weight, down_weight, probe_rows, probe_cols, moment):
    tok_count, features = tokens.shape
    own_rows, ff_held = up_weight.shape
    *sizes, cores = (lax.axis_size(name) for name in AXES)
    sizes = tuple(sizes)
    groups = sizes[1] * sizes[3]
    cols = ff_held // groups
    share = tok_count // cores
    col_keys = lax.dynamic_slice_in_dim(probe_cols, lax.axis_index(("b", "f")) * cols, cols)
    signs = probe_signs(probe_rows, col_keys)
    first = lax.axis_index("tensor") * share
    live_own = lax.dynamic_slice_in_dim(live_mask, first, share).astype(jnp.float32)[:, None]
    targets_own = lax.dynamic_slice_in_dim(targets, first, share)
    all_tokens, up_full, down_full = gather(sizes, tokens, up_weight, down_weight)
    all_tokens = all_tokens.reshape(-1, features)
    up_full = up_full.reshape(features, cols)
    down_full = down_full.reshape(features, cols)
    preact = jnp.dot(all_tokens, up_full, preferred_element_type=jnp.float32)
    tangent = jnp.dot(all_tokens, signs, preferred_element_type=jnp.float32)
    gelu_value, gelu_slope, gelu_curve = gelu_parts(preact)
    hidden = gelu_value.astype(jnp.bfloat16)
    hidden_dir = (gelu_slope * tangent).astype(jnp.bfloat16)
    dims = (((1,), (1,)), ((), ()))
    out_part = lax.dot_general(hidden, down_full, dims, preferred_element_type=jnp.float32).astype(jnp.bfloat16)
    dir_part = lax.dot_general(hidden_dir, down_full, dims, preferred_element_type=jnp.float32)
    split = (groups, cores, share, features)
    residual, tiles = exchange(sizes, cores, out_part.reshape(split), dir_part.reshape(split), targets_own, live_own)
    residual = residual.reshape(2, -1, features)
    tile = jnp.sum(tiles, axis=(0, 1))
    grads = jnp.einsum("ntd,df->ntf", residual, down_full, preferred_element_type=jnp.float32)
    chain_grad = (grads[1] * gelu_slope + grads[0] * gelu_curve * tangent).astype(jnp.bfloat16)
    product = jnp.einsum("tr,tf->rf", all_tokens, chain_grad, preferred_element_type=jnp.float32)
    blocks = cols // BLOCK
    row_halves = 2 if own_rows % 2 == 0 else 1
    column = lax.broadcasted_iota(jnp.int32, (cols, row_halves * blocks), 1)
    owner = lax.broadcasted_iota(jnp.int32, (cols, row_halves * blocks), 0) // BLOCK
    signed = (signs.astype(jnp.float32) * product).reshape(-1, row_halves, own_rows // row_halves, cols)
    summed = 0.0
    for half in range(row_halves):
        member = (owner + half * blocks == column).astype(jnp.float32)
        summed += jnp.einsum("hrf,fk->hrk", signed[:, half], member, precision=lax.Precision.HIGH)
    rows, sums = reduce_rows(sizes, summed.reshape(sizes + summed.shape[1:]), tile)
    loss_sum, total_count = sums[0, 0], sums[1, 0]
    summed = rows.reshape(groups, own_rows // row_halves, row_halves, blocks)
    summed = summed.transpose(2, 1, 0, 3).reshape(own_rows, groups * blocks)
    hess_diag = summed * (1.0 / BLOCK) / total_count
    second_moment = beta_two * moment + (1.0 - beta_two) * hess_diag * hess_diag
    mean_loss = loss_sum / (2.0 * total_count)
    return (hess_diag, second_moment, mean_loss)


def solution(mesh):
    dp = mesh.shape["dp"]
    cuts = (dp // 8, 2, 2, 2)
    split = Mesh(mesh.devices.reshape(cuts + (mesh.shape["tensor"],)), AXES)
    rows = AXES[:4]
    placed = (
        P(rows, None),
        P(rows, None),
        P(rows),
        P(rows, "tensor"),
        P(rows, "tensor"),
        P(),
        P("tensor"),
        P(rows, "tensor"),
    )
    return jax.shard_map(
        body,
        mesh=split,
        in_specs=placed,
        out_specs=(P(rows, "tensor"), P(rows, "tensor"), P()),
        check_vma=False,
    )
```

```python
import functools
import jax
import jax.numpy as jnp
from jax import lax
from jax.experimental import pallas as pl
from jax.experimental.pallas import tpu as pltpu
from jax.sharding import Mesh, PartitionSpec as P

BLOCK = 14

gelu_coef = 0.7978845608028654
cubic_coef = 0.044715
beta_two = 0.999


def probe_signs(row_keys, col_keys):
    hashed = jnp.bitwise_xor(row_keys[:, None] * 747796405, col_keys[None, :])
    hashed = jnp.bitwise_xor(hashed, jnp.right_shift(hashed, 15) & 131071)
    hashed = hashed * 695872825
    hashed = jnp.bitwise_xor(hashed, jnp.right_shift(hashed, 13) & 524287)
    hashed = hashed * 739982445
    hashed = jnp.bitwise_xor(hashed, jnp.right_shift(hashed, 16) & 65535)
    parity = jnp.right_shift(hashed, 11) & 1
    return (2 * parity - 1).astype(jnp.bfloat16)


def gelu_parts(preact):
    tanh_arg = gelu_coef * (preact + cubic_coef * preact * preact * preact)
    tanh_val = jnp.tanh(tanh_arg)
    sech_sq = 1.0 - tanh_val * tanh_val
    arg_slope = gelu_coef * (1.0 + 3.0 * cubic_coef * preact * preact)
    arg_curve = gelu_coef * 6.0 * cubic_coef * preact
    gelu_value = 0.5 * preact * (1.0 + tanh_val)
    gelu_slope = 0.5 * (1.0 + tanh_val) + 0.5 * preact * sech_sq * arg_slope
    gelu_curve = sech_sq * (
        arg_slope - preact * tanh_val * arg_slope * arg_slope + 0.5 * preact * arg_curve
    )
    return (gelu_value, gelu_slope, gelu_curve)


AXES = ("a", "b", "e", "f", "tensor")
MESH = pl.DeviceIdType.MESH
ANY = pl.BlockSpec(memory_space=pl.ANY)
VMEM = pl.BlockSpec(memory_space=pltpu.VMEM)


def remote(src, dst, send_sem, recv_sem, device):
    return pltpu.make_async_remote_copy(
        src_ref=src, dst_ref=dst, send_sem=send_sem, recv_sem=recv_sem, device_id=device, device_id_type=MESH
    )


def offsets(*sizes):
    found = [()]
    for size in sizes:
        found = [head + (step,) for head in found for step in range(size)]
    return found


def moved(at, step, size, way):
    return lax.rem(at + step if way > 0 else at + size - step, size)


def gather_kernel(
    sizes, tok_ref, up_ref, down_ref, tok_all, up_all, down_all,
    own_sem, tok_send, tok_recv, pass_send, pass_recv, swap_send, swap_recv, far_send, far_recv, near_send, near_recv,
):
    na, nb, ne, nf = sizes
    a, b, e, f, c = (lax.axis_index(name) for name in AXES)
    cols = up_all.shape[5]
    plane = offsets(nb, nf)
    barrier = pltpu.get_barrier_semaphore()

    def peer(d, way):
        return (a, moved(b, plane[d][0], nb, way), e, moved(f, plane[d][1], nf, way), c)

    def far(s, way):
        return (moved(a, s, na, way), b, e, f, c)

    def near(t, way):
        return (a, b, moved(e, t, ne, way), f, c)

    friends = [peer(d, 1) for d in range(1, len(plane))]
    friends += [far(s, 1) for s in range(1, na)] + [near(t, 1) for t in range(1, ne)]
    twin = (a, b, e, f, 1 - c)
    friends.append(twin)
    for place in friends:
        pl.semaphore_signal(barrier, inc=1, device_id=place, device_id_type=MESH)
    pl.semaphore_wait(barrier, len(friends))

    held = ((up_ref, up_all), (down_ref, down_all))

    def cut(w, place):
        return held[w][0].at[:, pl.ds(pl.multiple_of((place[1] * nf + place[3]) * cols, cols), cols)]

    def swap(w, d):
        to = peer(d, 1)
        sems = swap_send.at[w, d - 1], swap_recv.at[w, d - 1]
        return remote(cut(w, to), held[w][1].at[a, b, e, f], *sems, to)

    def swapped(w, d):
        came = peer(d, -1)
        sems = swap_send.at[w, d - 1], swap_recv.at[w, d - 1]
        return remote(cut(w, came), held[w][1].at[a, came[1], e, came[3]], *sems, came)

    def token(d, way):
        place = peer(d, way)
        slot = tok_all.at[b, f, c] if way > 0 else tok_all.at[place[1], place[3], c]
        return remote(tok_ref.at[c], slot, tok_send.at[d - 1], tok_recv.at[d - 1], place)

    def token_pass(d, core):
        came = peer(d, -1)
        slot = tok_all.at[came[1], came[3], core]
        return remote(slot, slot, pass_send.at[d - 1], pass_recv.at[d - 1], twin)

    def chunk(w, d, at_a, at_e):
        came = peer(d, -1)
        return held[w][1].at[at_a, came[1], at_e, came[3]]

    def far_hop(w, d, s, way):
        slot = chunk(w, d, a if way > 0 else moved(a, s, na, -1), e)
        return remote(slot, slot, far_send.at[w, d, s - 1], far_recv.at[w, d, s - 1], far(s, way))

    def near_hop(w, d, s, t, way):
        slot = chunk(w, d, moved(a, s, na, -1), e if way > 0 else moved(e, t, ne, -1))
        return remote(slot, slot, near_send.at[w, d, s, t - 1], near_recv.at[w, d, s, t - 1], near(t, way))

    owns = [pltpu.make_async_copy(cut(w, (a, b, e, f)), held[w][1].at[a, b, e, f], own_sem.at[w]) for w in range(2)]
    owns.append(pltpu.make_async_copy(tok_ref, tok_all.at[b, f], own_sem.at[2]))
    for copy in owns:
        copy.start()
    for d in range(1, len(plane)):
        swap(0, d).start()
    for d in range(1, len(plane)):
        swap(1, d).start()
    for d in range(1, len(plane)):
        token(d, 1).start()
    for w in range(2):
        for d in range(len(plane)):
            if d == 0:
                owns[w].wait()
            else:
                swapped(w, d).wait_recv()

            @pl.loop(1, na)
            def _(s):
                far_hop(w, d, s, 1).start()

            for t in range(1, ne):
                near_hop(w, d, 0, t, 1).start()
    for d in range(1, len(plane)):
        token(d, -1).wait_recv()
        token_pass(d, c).start()
    for w in range(2):
        for d in range(len(plane)):
            @pl.loop(1, na)
            def _(s):
                far_hop(w, d, s, -1).wait_recv()
                for t in range(1, ne):
                    near_hop(w, d, s, t, 1).start()

    owns[2].wait()
    for d in range(1, len(plane)):
        token_pass(d, 1 - c).wait_recv()
        token_pass(d, c).wait_send()
        token(d, 1).wait_send()
    for w in range(2):
        for d in range(1, len(plane)):
            swap(w, d).wait_send()
        for d in range(len(plane)):
            @pl.loop(0, na)
            def _(s):
                for t in range(1, ne):
                    near_hop(w, d, s, t, -1).wait_recv()
                    near_hop(w, d, s, t, 1).wait_send()

            @pl.loop(1, na)
            def _(s):
                far_hop(w, d, s, 1).wait_send()


def gather(sizes, tokens, up_weight, down_weight):
    na, nb, ne, nf = sizes
    own_rows, ff_held = up_weight.shape
    groups = nb * nf
    full = jax.ShapeDtypeStruct(sizes + (own_rows, ff_held // groups), up_weight.dtype)
    dma = pltpu.SemaphoreType.DMA
    return pl.pallas_call(
        functools.partial(gather_kernel, sizes),
        name="gather",
        out_shape=(jax.ShapeDtypeStruct((nb, nf) + tokens.shape, tokens.dtype), full, full),
        in_specs=[ANY] * 3,
        out_specs=(ANY,) * 3,
        scratch_shapes=[
            dma((3,)), *[dma((groups - 1,))] * 4, dma((2, groups - 1)), dma((2, groups - 1)),
            dma((2, groups, na - 1)), dma((2, groups, na - 1)),
            dma((2, groups, na, ne - 1)), dma((2, groups, na, ne - 1)),
        ],
        compiler_params=pltpu.CompilerParams(collective_id=0, has_side_effects=True),
    )(tokens, up_weight, down_weight)


def residual_kernel(
    sizes, cores, out_ref, dir_ref, targets_ref, live_ref, res_all, tile_all,
    half_out, half_dir, send_out, send_dir, got_out, got_dir,
    half_send, half_recv, part_send, part_recv, res_send, res_recv, pass_send, pass_recv, tile_send, tile_recv,
):
    na, nb, ne, nf = sizes
    a, b, e, f, c = (lax.axis_index(name) for name in AXES)
    plane = offsets(nb, nf)
    groups = len(plane)
    twin = 1 - c
    g = b * nf + f
    twin_at = (a, b, e, f, twin)
    barrier = pltpu.get_barrier_semaphore()
    others = [(d, k) for d in range(groups) for k in range(cores) if (d, k) != (0, 0)]

    def at(d, k, way=1):
        return (a, moved(b, plane[d][0], nb, way), e, moved(f, plane[d][1], nf, way), moved(c, k, cores, way))

    def back(d, k):
        return at(d, k, -1)

    def spot(d, way):
        place = at(d, 0, way)
        return place[1] * nf + place[3]

    for d, k in others:
        pl.semaphore_signal(barrier, inc=1, device_id=at(d, k), device_id_type=MESH)
    pl.semaphore_wait(barrier, len(others))

    def halves(d):
        to = spot(d, 1)
        return (
            remote(out_ref.at[to, twin], half_out.at[d], half_send.at[0, d], half_recv.at[0, d], twin_at),
            remote(dir_ref.at[to, twin], half_dir.at[d], half_send.at[1, d], half_recv.at[1, d], twin_at),
        )

    def parts(d):
        return (
            remote(send_out.at[d], got_out.at[d - 1], part_send.at[0, d - 1], part_recv.at[0, d - 1], at(d, 0)),
            remote(send_dir.at[d], got_dir.at[d - 1], part_send.at[1, d - 1], part_recv.at[1, d - 1], at(d, 0)),
        )

    order = list(range(1, groups)) + [0]
    for d in order:
        for copy in halves(d):
            copy.start()
    for d in order:
        to = spot(d, 1)
        for copy in halves(d):
            copy.wait_recv()
        total = out_ref[to, c].astype(jnp.float32) + half_out[d].astype(jnp.float32)
        send_out[d] = total.astype(jnp.bfloat16)
        send_dir[d] = dir_ref[to, c] + half_dir[d]
        if d:
            for copy in parts(d):
                copy.start()
    outputs = total
    out_dir = send_dir[0]
    for d in range(1, groups):
        for copy in parts(d):
            copy.wait_recv()
        outputs += got_out[d - 1].astype(jnp.float32)
        out_dir += got_dir[d - 1]
    live = live_ref[...]
    diff = outputs - targets_ref[...].astype(jnp.float32)
    weighted = live * diff
    res_all[0, g, c] = weighted.astype(jnp.bfloat16)
    res_all[1, g, c] = (live * out_dir).astype(jnp.bfloat16)
    loss = jnp.sum(weighted * diff, keepdims=True)
    count = jnp.sum(live, keepdims=True)
    tile_all[g, c] = jnp.where(lax.broadcasted_iota(jnp.int32, tile_all.shape[2:], 0) == 0, loss, count)

    def sent(d):
        slot = res_all.at[:, g, c]
        return remote(slot, slot, res_send.at[d], res_recv.at[d], at(d, 0) if d else twin_at)

    def received(d):
        slot = res_all.at[:, spot(d, -1), c] if d else res_all.at[:, g, twin]
        return remote(slot, slot, res_send.at[d], res_recv.at[d], back(d, 0) if d else twin_at)

    def passed(d, core):
        slot = res_all.at[:, spot(d, -1), core]
        return remote(slot, slot, pass_send.at[d - 1], pass_recv.at[d - 1], twin_at)

    def tile(i, source, place):
        slot = tile_all.at[source[1] * nf + source[3], source[4]]
        return remote(slot, slot, tile_send.at[i], tile_recv.at[i], place)

    for d in order:
        sent(d).start()
    for i, (d, k) in enumerate(others):
        tile(i, (a, b, e, f, c), at(d, k)).start()
    for d in range(1, groups):
        received(d).wait_recv()
        passed(d, c).start()
    received(0).wait_recv()
    for i, (d, k) in enumerate(others):
        tile(i, back(d, k), back(d, k)).wait_recv()
    for d in range(1, groups):
        passed(d, twin).wait_recv()
    for d in range(groups):
        for copy in halves(d):
            copy.wait_send()
        sent(d).wait_send()
        if d:
            for copy in parts(d):
                copy.wait_send()
            passed(d, c).wait_send()
    for i, (d, k) in enumerate(others):
        tile(i, (a, b, e, f, c), at(d, k)).wait_send()


def exchange(sizes, cores, out_part, dir_part, targets, live):
    groups = sizes[1] * sizes[3]
    share, features = targets.shape
    dma = pltpu.SemaphoreType.DMA
    bf, f32 = jnp.bfloat16, jnp.float32
    return pl.pallas_call(
        functools.partial(residual_kernel, sizes, cores),
        name="residual",
        out_shape=(
            jax.ShapeDtypeStruct((2, groups, cores, share, features), bf),
            jax.ShapeDtypeStruct((groups, cores, 8, 128), f32),
        ),
        in_specs=[VMEM] * 4,
        out_specs=(VMEM,) * 2,
        scratch_shapes=[
            pltpu.VMEM((groups, share, features), bf), pltpu.VMEM((groups, share, features), f32),
            pltpu.VMEM((groups, share, features), bf), pltpu.VMEM((groups, share, features), f32),
            pltpu.VMEM((groups - 1, share, features), bf), pltpu.VMEM((groups - 1, share, features), f32),
            dma((2, groups)), dma((2, groups)), dma((2, groups - 1)), dma((2, groups - 1)),
            dma((groups,)), dma((groups,)), dma((groups - 1,)), dma((groups - 1,)),
            dma((groups * cores - 1,)), dma((groups * cores - 1,)),
        ],
        compiler_params=pltpu.CompilerParams(collective_id=1, has_side_effects=True),
    )(out_part, dir_part, targets, live)


def reduce_kernel(
    sizes, part_ref, tile_ref, out_ref, sums_ref, got, got_tile, total,
    line_send, line_recv, tile_send, tile_recv, swap_send, swap_recv,
):
    na, nb, ne, nf = sizes
    a, b, e, f, c = (lax.axis_index(name) for name in AXES)
    plane, fans = offsets(nb, nf), offsets(na, ne)
    barrier = pltpu.get_barrier_semaphore()

    def peer(d, way):
        return (a, moved(b, plane[d][0], nb, way), e, moved(f, plane[d][1], nf, way), c)

    def fan(s):
        return (moved(a, fans[s][0], na, 1), b, moved(e, fans[s][1], ne, 1), f, c)

    friends = [peer(d, 1) for d in range(1, len(plane))] + [fan(s) for s in range(1, len(fans))]
    for place in friends:
        pl.semaphore_signal(barrier, inc=1, device_id=place, device_id_type=MESH)
    pl.semaphore_wait(barrier, len(friends))

    def line(s):
        to = fan(s)
        return (
            remote(part_ref.at[to[0], :, to[2]], got.at[s - 1], line_send.at[s - 1], line_recv.at[s - 1], to),
            remote(tile_ref, got_tile.at[s - 1], tile_send.at[s - 1], tile_recv.at[s - 1], to),
        )

    def swap(d, way):
        place = peer(d, way)
        slot = out_ref.at[b, f] if way > 0 else out_ref.at[place[1], place[3]]
        return remote(total.at[place[1], place[3]], slot, swap_send.at[d - 1], swap_recv.at[d - 1], place)

    for s in range(1, len(fans)):
        for copy in line(s):
            copy.start()
    acc = part_ref[a, :, e]
    sums = tile_ref[...]
    for s in range(1, len(fans)):
        for copy in line(s):
            copy.wait_recv()
        acc += got[s - 1]
        sums += got_tile[s - 1]
    total[...] = acc
    sums_ref[...] = sums
    for d in range(1, len(plane)):
        swap(d, 1).start()
    out_ref[b, f] = total[b, f]
    for d in range(1, len(plane)):
        swap(d, -1).wait_recv()
    for d in range(1, len(plane)):
        swap(d, 1).wait_send()
    for s in range(1, len(fans)):
        for copy in line(s):
            copy.wait_send()


def reduce_rows(sizes, part, tile):
    na, nb, ne, nf = sizes
    dma = pltpu.SemaphoreType.DMA
    shape = (nb, nf) + part.shape[4:]
    peers, groups = na * ne - 1, nb * nf
    return pl.pallas_call(
        functools.partial(reduce_kernel, sizes),
        name="reduce_rows",
        out_shape=(jax.ShapeDtypeStruct(shape, part.dtype), jax.ShapeDtypeStruct(tile.shape, tile.dtype)),
        in_specs=[VMEM] * 2,
        out_specs=(VMEM,) * 2,
        scratch_shapes=[
            pltpu.VMEM((peers,) + shape, part.dtype), pltpu.VMEM((peers,) + tile.shape, tile.dtype),
            pltpu.VMEM(shape, part.dtype),
            dma((peers,)), dma((peers,)), dma((peers,)), dma((peers,)), dma((groups - 1,)), dma((groups - 1,)),
        ],
        compiler_params=pltpu.CompilerParams(collective_id=2, has_side_effects=True),
    )(part, tile)


def body(tokens, targets, live_mask, up_weight, down_weight, probe_rows, probe_cols, moment):
    tok_count, features = tokens.shape
    own_rows, ff_held = up_weight.shape
    *sizes, cores = (lax.axis_size(name) for name in AXES)
    sizes = tuple(sizes)
    groups = sizes[1] * sizes[3]
    cols = ff_held // groups
    share = tok_count // cores
    col_keys = lax.dynamic_slice_in_dim(probe_cols, lax.axis_index(("b", "f")) * cols, cols)
    signs = probe_signs(probe_rows, col_keys)
    first = lax.axis_index("tensor") * share
    live_own = lax.dynamic_slice_in_dim(live_mask, first, share).astype(jnp.float32)[:, None]
    targets_own = lax.dynamic_slice_in_dim(targets, first, share)
    all_tokens, up_full, down_full = gather(sizes, tokens.reshape(cores, share, features), up_weight, down_weight)
    all_tokens = all_tokens.reshape(-1, features)
    up_full = up_full.reshape(features, cols)
    down_full = down_full.reshape(features, cols)
    preact = jnp.dot(all_tokens, up_full, preferred_element_type=jnp.float32)
    tangent = jnp.dot(all_tokens, signs, preferred_element_type=jnp.float32)
    gelu_value, gelu_slope, gelu_curve = gelu_parts(preact)
    hidden = gelu_value.astype(jnp.bfloat16)
    hidden_dir = (gelu_slope * tangent).astype(jnp.bfloat16)
    dims = (((1,), (1,)), ((), ()))
    out_part = lax.dot_general(hidden, down_full, dims, preferred_element_type=jnp.float32).astype(jnp.bfloat16)
    dir_part = lax.dot_general(hidden_dir, down_full, dims, preferred_element_type=jnp.float32)
    split = (groups, cores, share, features)
    residual, tiles = exchange(sizes, cores, out_part.reshape(split), dir_part.reshape(split), targets_own, live_own)
    residual = residual.reshape(2, -1, features)
    tile = jnp.sum(tiles, axis=(0, 1))
    grads = jnp.einsum("ntd,df->ntf", residual, down_full, preferred_element_type=jnp.float32)
    chain_grad = (grads[1] * gelu_slope + grads[0] * gelu_curve * tangent).astype(jnp.bfloat16)
    product = jnp.einsum("tr,tf->rf", all_tokens, chain_grad, preferred_element_type=jnp.float32)
    blocks = cols // BLOCK
    row_halves = 2 if own_rows % 2 == 0 else 1
    column = lax.broadcasted_iota(jnp.int32, (cols, row_halves * blocks), 1)
    owner = lax.broadcasted_iota(jnp.int32, (cols, row_halves * blocks), 0) // BLOCK
    signed = (signs.astype(jnp.float32) * product).reshape(-1, row_halves, own_rows // row_halves, cols)
    summed = 0.0
    for half in range(row_halves):
        member = (owner + half * blocks == column).astype(jnp.float32)
        summed += jnp.einsum("hrf,fk->hrk", signed[:, half], member, precision=lax.Precision.HIGH)
    rows, sums = reduce_rows(sizes, summed.reshape(sizes + summed.shape[1:]), tile)
    loss_sum, total_count = sums[0, 0], sums[1, 0]
    summed = rows.reshape(groups, own_rows // row_halves, row_halves, blocks)
    summed = summed.transpose(2, 1, 0, 3).reshape(own_rows, groups * blocks)
    hess_diag = summed * (1.0 / BLOCK) / total_count
    second_moment = beta_two * moment + (1.0 - beta_two) * hess_diag * hess_diag
    mean_loss = loss_sum / (2.0 * total_count)
    return (hess_diag, second_moment, mean_loss)


def solution(mesh):
    dp = mesh.shape["dp"]
    cuts = (dp // 8, 2, 2, 2)
    split = Mesh(mesh.devices.reshape(cuts + (mesh.shape["tensor"],)), AXES)
    rows = AXES[:4]
    placed = (
        P(rows, None),
        P(rows, None),
        P(rows),
        P(rows, "tensor"),
        P(rows, "tensor"),
        P(),
        P("tensor"),
        P(rows, "tensor"),
    )
    return jax.shard_map(
        body,
        mesh=split,
        in_specs=placed,
        out_specs=(P(rows, "tensor"), P(rows, "tensor"), P()),
        check_vma=False,
    )
```
